32 devices in a mesh: dp: 4 (over y, x), expert: 8 (over z, core).
Axes of the slice: x: 2, y: 2, z: 4, core: 2. Of those that a mesh axis runs over, the one named last changes fastest.
Arguments:
- tokens: bfloat16 [4096, 1024], P(('dp', 'expert')), may hold values from -6 to 6
- expert_ids: int32 [4096, 4], P(('dp', 'expert')), may hold values from 0 to 7, all different within a row; in each aligned block of 128 rows (0 to 127, 128 to 255, ...) at most 96 rows name the same one
- gate_probs: float32 [4096, 4], P(('dp', 'expert')), may hold values from 0.05 to 0.6
- w_gate: bfloat16 [8, 1024, 512], P('expert', 'dp'), may hold values from -0.1875 to 0.1875
- w_up: bfloat16 [8, 1024, 512], P('expert', 'dp'), may hold values from -0.1875 to 0.1875
- w_down: bfloat16 [8, 512, 1024], P('expert', 'dp'), may hold values from -0.25 to 0.25
- cotangent: bfloat16 [4096, 1024], P(('dp', 'expert')), may hold values from -6 to 6
Outputs:
- mixed: bfloat16 [4096, 1024], P(('dp', 'expert'))
- input_grad: bfloat16 [4096, 1024], P(('dp', 'expert'))
- prob_grad: float32 [4096, 4], P(('dp', 'expert'))
- gate_grad: bfloat16 [8, 1024, 512], P('expert', 'dp')
- up_grad: bfloat16 [8, 1024, 512], P('expert', 'dp')
- down_grad: bfloat16 [8, 512, 1024], P('expert', 'dp')
The draws below stay inside these ranges and needn't reach their ends.
Inputs may be any that keep to these rules, and one draw needn't show every extreme that they name: `expert_ids`: each row names 4 different experts. Among the rows of one device no expert is named more than 96 times, and in every draw some expert is named exactly 96 times by the rows of some device.
All inputs are finite; a program needn't handle non-finite values.
Results may differ from the reference program's by a relative error of at most 0.015.
Values may be sent and summed in bfloat16 or wider, within the bound.
No kernel may reach another device: no remote copies, remote signals or barrier semaphores. Data moves between devices by JAX's collectives and lax.ppermute only.
A program may use at most 64 MiB of HBM per device.

```python
import math
import jax
import jax.numpy as jnp
import numpy as np
from jax import lax

D = 1024
FF = 512
TOP = 4
TOK_DEV = 128
EXPERTS = 8
TOKENS = 4096
CAP = 96
N_DP = 4
N_EXPERT = 8


def block_scale(own_key, extent, shards, low, high):
    def one(axis_at, shards_of):
        heights = jax.random.uniform(jax.random.fold_in(jax.random.fold_in(own_key, 6), axis_at), (shards_of,), jnp.float32, low / len(shards), high / len(shards))
        return jnp.repeat(jnp.exp(heights), extent[axis_at] // shards_of).reshape((-1,) + (1,) * (len(extent) - axis_at - 1))

    gain = one(*shards[0])
    for cut in shards[1:]:
        gain = gain * one(*cut)
    return gain


def deal_out(stream_key, own, number, rows, number_of, top, limit, slope):
    order = jax.random.permutation(stream_key, number_of)
    crowded, common = shares(number_of, rows * top, limit, slope, True), shares(number_of, rows * top, limit, slope, False)
    places = jnp.arange(number_of)

    def named(sizes, turn):
        used = int((sizes > 0).sum())
        fixed = max(1, used // 4)
        shifted = fixed + (places - fixed + turn * (used - fixed)) % max(1, number_of - fixed)
        return jnp.zeros((number_of,), jnp.int32).at[order[jnp.where(places < fixed, places, shifted)]].set(jnp.asarray(sizes, jnp.int32))

    sizes = jnp.where(number % 4 == 0, named(crowded, number // 4), named(common, number - number // 4 - 1))
    mixed = jax.random.permutation(jax.random.fold_in(own, 3), number_of)
    source_of, taker = mixed[0:number_of // 2 * 2:2], mixed[1:number_of // 2 * 2:2]
    room = jnp.minimum(sizes[source_of] - 1, limit - sizes[taker]) // 2
    room = jnp.where((source_of == order[0]) | (taker == order[0]) | (sizes[taker] == 0), 0, jnp.maximum(room, 0))
    shifted = jax.random.randint(jax.random.fold_in(own, 4), (number_of // 2,), 0, 1 << 20) % (room + 1)
    sizes = sizes.at[source_of].add(-shifted).at[taker].add(shifted)
    items = jnp.searchsorted(jnp.cumsum(sizes), jnp.arange(rows * top), side="right").astype(jnp.int32)
    grid = items.reshape(top, rows).T
    grid = grid[jax.random.permutation(jax.random.fold_in(own, 1), rows)]
    turn = jax.random.randint(jax.random.fold_in(own, 2), (rows, 1), 0, top)
    return jnp.take_along_axis(grid, (jnp.arange(top)[None, :] + turn) % top, axis=1)


def shares(count, total, most, lean, full):
    weights = [(1 << 20) // math.isqrt(standing ** lean) + 1 for standing in range(1, count + 1)]
    largest = most if full else min(most, max(-(-total // count), total * weights[0] // sum(weights)))
    least = 1 if total - largest >= count - 1 else 0
    holding, spare = [largest] + [least] * (count - 1), total - largest - least * (count - 1)
    while spare > 0:
        free = [i for i in range(1, count) if holding[i] < largest] or [i for i in range(1, count) if holding[i] < most]
        pool, remaining = sum([weights[i] for i in free]), spare
        for i in free:
            more = min(most - holding[i], max(1, remaining * weights[i] // pool), spare)
            holding[i] = holding[i] + more
            spare = spare - more
    return np.array(holding)


def noise(rng, dims, spread, reach, shards=(), kind=jnp.bfloat16):
    entries = spread * jax.random.normal(rng, dims, jnp.float32)
    if shards:
        entries = entries * block_scale(rng, dims, shards, -0.22, 0.18)
    return jnp.clip(entries, -reach, reach).astype(kind)


def setup_inputs(seed: int = 0) -> dict:
    seeds = jax.random.split(jax.random.key(seed), 8)
    tokens = noise(seeds[0], (TOKENS, D), 1.0, 6.0, ((0, 32),))
    expert_ids_keys = jax.random.split(jax.random.fold_in(seeds[1], 1), TOKENS // TOK_DEV)
    expert_ids_turns = jax.random.permutation(jax.random.fold_in(seeds[1], 3), TOKENS // TOK_DEV)
    expert_ids = jax.vmap(lambda own, number: deal_out(jax.random.fold_in(seeds[1], 2), own, number, TOK_DEV, EXPERTS, TOP, CAP, 2))(expert_ids_keys, expert_ids_turns).reshape((TOKENS, TOP))
    gate_probs = jnp.clip(0.05 + 0.55 * jax.random.uniform(seeds[2], (TOKENS, TOP), jnp.float32) ** block_scale(seeds[2], (TOKENS, TOP), ((0, 32),), -0.2, 0.2), 0.05, 0.6)
    w_gate = noise(seeds[3], (EXPERTS, D, FF), D ** -0.5, 0.1875, ((0, 8), (1, 4)))
    w_up = noise(seeds[4], (EXPERTS, D, FF), D ** -0.5, 0.1875, ((0, 8), (1, 4)))
    w_down = noise(seeds[5], (EXPERTS, FF, D), FF ** -0.5, 0.25, ((0, 8), (1, 4)))
    cotangent = noise(seeds[6], (TOKENS, D), 1.0, 6.0, ((0, 32),))
    return {"tokens": tokens, "expert_ids": expert_ids, "gate_probs": gate_probs, "w_gate": w_gate, "w_up": w_up, "w_down": w_down, "cotangent": cotangent}


def slot_table(block_ids):
    pair_count = block_ids.shape[0]
    onehot = (block_ids[:, None] == jnp.arange(EXPERTS, dtype=jnp.int32)[None, :]).astype(jnp.int32)
    slot_rank = lax.optimization_barrier(jnp.sum((jnp.cumsum(onehot, axis=0) - 1) * onehot, axis=1))
    target = (block_ids * CAP + slot_rank).astype(jnp.int32)
    empty_table = jnp.full((EXPERTS * CAP,), pair_count, jnp.int32)
    return empty_table.at[target].set(jnp.arange(pair_count, dtype=jnp.int32))

def pick_rows(table, index):
    return table[index]

def add_rows(total, index, values):
    return total.at[index].add(values)

def weight_grad(rows_in, grads_in, grad_scale):
    term = jnp.einsum('irk,irf->ikf', rows_in.astype(jnp.float32), grads_in.astype(jnp.float32)) * grad_scale
    term = lax.optimization_barrier(term.astype(jnp.bfloat16))
    return lax.optimization_barrier(jnp.sum(term.astype(jnp.float32), axis=0)).astype(jnp.bfloat16)

def reference(tokens, expert_ids, gate_probs, w_gate, w_up, w_down, cotangent):
    blocks = TOKENS // TOK_DEV
    pair_count = TOK_DEV * TOP
    slot_owner = lax.map(slot_table, expert_ids.reshape(blocks, pair_count).astype(jnp.int32))
    zero_rows = jnp.zeros((blocks, 1, D), tokens.dtype)
    padded_tokens = jnp.concatenate([tokens.reshape(blocks, TOK_DEV, D), zero_rows], axis=1)
    padded_cot = jnp.concatenate([cotangent.reshape(blocks, TOK_DEV, D), zero_rows], axis=1)
    padded_probs = jnp.concatenate([gate_probs.reshape(blocks, pair_count), jnp.zeros((blocks, 1), gate_probs.dtype)], axis=1)
    grad_scale = (EXPERTS / (TOKENS * TOP)) ** 0.5
    picker = jax.vmap(pick_rows)
    adder = jax.vmap(add_rows)
    dp_shape = (N_DP, N_EXPERT * CAP)

    def per_expert(totals, expert):
        mixed_total, input_total, prob_total = totals
        owner_here = lax.dynamic_slice_in_dim(slot_owner, expert * CAP, CAP, 1)
        token_rows = jnp.where(owner_here < pair_count, owner_here // TOP, TOK_DEV).astype(jnp.int32)
        rows_in = picker(padded_tokens, token_rows).reshape(blocks * CAP, D)
        prob_in = picker(padded_probs, owner_here).reshape(blocks * CAP, 1).astype(jnp.float32)
        cot_in = picker(padded_cot, token_rows).reshape(blocks * CAP, D)
        gate_w = w_gate[expert]
        up_w = w_up[expert]
        down_w = w_down[expert]
        gate_pre = jnp.dot(rows_in, gate_w, preferred_element_type=jnp.float32)
        up_pre = jnp.dot(rows_in, up_w, preferred_element_type=jnp.float32)
        hidden = (jax.nn.silu(gate_pre) * up_pre).astype(jnp.bfloat16)
        result = jnp.dot(hidden, down_w, preferred_element_type=jnp.float32).astype(jnp.bfloat16)
        result_wide = result.astype(jnp.float32)
        cot_wide = cot_in.astype(jnp.float32)
        mixed_total = adder(mixed_total, token_rows, (prob_in * result_wide).reshape(blocks, CAP, D))
        prob_total = adder(prob_total, owner_here, lax.optimization_barrier(jnp.sum(cot_wide * result_wide, axis=1)).reshape(blocks, CAP))
        out_grad = (prob_in * cot_wide).astype(jnp.bfloat16)
        hidden_grad = jnp.dot(out_grad, down_w.T, preferred_element_type=jnp.float32)
        sigmoid_gate = jax.nn.sigmoid(gate_pre)
        up_grad_pre = (hidden_grad * jax.nn.silu(gate_pre)).astype(jnp.bfloat16)
        gate_grad_pre = (hidden_grad * up_pre * sigmoid_gate * (1.0 + gate_pre * (1.0 - sigmoid_gate))).astype(jnp.bfloat16)
        row_grad = (jnp.dot(gate_grad_pre, gate_w.T, preferred_element_type=jnp.float32) + jnp.dot(up_grad_pre, up_w.T, preferred_element_type=jnp.float32)).astype(jnp.bfloat16)
        input_total = adder(input_total, token_rows, row_grad.astype(jnp.float32).reshape(blocks, CAP, D))
        rows_dp = rows_in.reshape(dp_shape + (D,))
        gate_part = weight_grad(rows_dp, gate_grad_pre.reshape(dp_shape + (FF,)), grad_scale)
        up_part = weight_grad(rows_dp, up_grad_pre.reshape(dp_shape + (FF,)), grad_scale)
        down_part = weight_grad(hidden.reshape(dp_shape + (FF,)), out_grad.reshape(dp_shape + (D,)), grad_scale)
        return ((mixed_total, input_total, prob_total), (gate_part, up_part, down_part))
    start = (jnp.zeros((blocks, TOK_DEV + 1, D), jnp.float32), jnp.zeros((blocks, TOK_DEV + 1, D), jnp.float32), jnp.zeros((blocks, pair_count + 1), jnp.float32))
    totals, grads = lax.scan(per_expert, start, jnp.arange(EXPERTS, dtype=jnp.int32))
    mixed_total, input_total, prob_total = totals
    mixed = mixed_total[:, :TOK_DEV].reshape(TOKENS, D).astype(jnp.bfloat16)
    input_grad = input_total[:, :TOK_DEV].reshape(TOKENS, D).astype(jnp.bfloat16)
    prob_grad = prob_total[:, :pair_count].reshape(TOKENS, TOP)
    return (mixed, input_grad, prob_grad, grads[0], grads[1], grads[2])
```

```python
import jax
import jax.numpy as jnp
from jax import lax
from jax.sharding import PartitionSpec as P

BF = jnp.bfloat16
F32 = jnp.float32


def send(x, axis, flip, only=None):
    size = lax.axis_size(axis)
    pairs = [(j, j ^ flip) for j in range(size) if only is None or only(j, j ^ flip)]
    return lax.ppermute(x, axis, pairs)


def spread(block):
    pairs = lax.axis_size("expert") // 2
    if pairs == 4:
        inner = lambda a, b: a // 2 in (1, 2)
        two = send(block, "expert", 4)
        one = send(block, "expert", 2)
        mid = send(block, "expert", 6, inner)
        far = send(two, "expert", 2, lambda a, b: a // 2 in (1, 2))
        row = lax.axis_index("expert") // 2
        three = jnp.where((row == 1) | (row == 2), mid, far)
        mine = [block, one, two, three]
    else:
        mine = [block] + [send(block, "expert", 2 * m) for m in range(1, pairs)]
    mine = lax.optimization_barrier(jnp.concatenate(mine, axis=0))
    return mine, send(mine, "expert", 1)


def collect(mine, other, rows):
    pairs = lax.axis_size("expert") // 2
    got = send(other, "expert", 1)
    total = (mine.astype(F32) + got.astype(F32)).astype(BF)
    total = lax.optimization_barrier(total)
    parts = [total[m * rows : (m + 1) * rows] for m in range(pairs)]
    out = parts[0].astype(F32)
    for m in range(1, pairs):
        out = out + send(parts[m], "expert", 2 * m).astype(F32)
    return out.astype(BF)


def in_order(parts, own):
    parts = list(parts)
    step = 1
    while step < len(parts):
        odd = (own & step) != 0
        parts = [jnp.where(odd, parts[j ^ step], parts[j]) for j in range(len(parts))]
        step *= 2
    return parts


def gather_rows(shard):
    size = lax.axis_size("dp")
    if size > 8:
        full = lax.all_gather(shard, "dp", axis=0, tiled=False)
        own = lax.axis_index("dp")
        return [lax.dynamic_index_in_dim(full, own ^ m, 0, False) for m in range(size)]
    parts = [shard]
    for m in range(1, size if size != 4 else 3):
        parts.append(send(shard, "dp", m))
    if size == 4:
        half = shard.shape[0] // 2
        lo = send(parts[2][:half], "dp", 1)
        hi = send(parts[1][half:], "dp", 2)
        parts.append(jnp.concatenate([lo, hi], axis=0))
    return parts


def scatter_rows(parts):
    size = lax.axis_size("dp")
    if size > 8:
        whole = jnp.concatenate(in_order(parts, lax.axis_index("dp")))
        return lax.psum_scatter(whole, "dp", scatter_dimension=0, tiled=True)
    total = parts[0].astype(F32)
    for m in range(1, size):
        total = total + send(parts[m], "dp", m).astype(F32)
    return total.astype(BF)


def mm(a, b, dims):
    return lax.dot_general(a, b, ((dims[0], dims[1]), ((), ())), preferred_element_type=F32)


def per_device(tokens, expert_ids, gate_probs, w_gate, w_up, w_down, cotangent):
    rows, width = tokens.shape
    top = expert_ids.shape[1]
    hid = w_gate.shape[2]
    expert_devices = lax.axis_size("expert")
    data_devices = lax.axis_size("dp")
    pairs = expert_devices // 2
    experts = expert_devices
    assert w_gate.shape[0] == 1
    scale = (experts / (rows * top * data_devices * expert_devices)) ** 0.5
    me = lax.axis_index("expert")
    own = lax.axis_index("dp")
    dwidth = width // data_devices
    dhid = hid // data_devices

    def shuffle(x):
        cols = [x[:, j * dwidth : (j + 1) * dwidth] for j in range(data_devices)]
        return jnp.concatenate(in_order(cols, own), axis=1)

    chosen = expert_ids.T[None, :, :] == jnp.arange(experts, dtype=jnp.int32)[:, None, None]
    dense = jnp.sum(jnp.where(chosen, gate_probs.T[None, :, :], 0.0), axis=1)
    x0, x1 = spread(shuffle(tokens))
    pair = jnp.concatenate([w_gate[0], w_up[0]], axis=1)
    wgu = gather_rows(pair)
    wgu = lax.optimization_barrier(jnp.concatenate(wgu, axis=0))
    wd = gather_rows(w_down[0])
    wd = lax.optimization_barrier(jnp.concatenate(in_order(wd, own), axis=0))
    c0, c1 = spread(cotangent)
    near = [dense]
    for m in range(1, pairs):
        near.append(send(dense, "expert", 2 * m))
    near = lax.optimization_barrier(jnp.stack(near))
    far = send(near, "expert", 1)
    p0 = lax.dynamic_index_in_dim(near, me, 1, False).reshape(pairs * rows, 1)
    p1 = lax.dynamic_index_in_dim(far, me, 1, False).reshape(pairs * rows, 1)

    def project(x):
        return lax.optimization_barrier(mm(x, wgu, ((1,), (0,))))

    def forward(pre, p):
        hidden = (jax.nn.silu(pre[:, :hid]) * pre[:, hid:]).astype(BF)
        result = mm(hidden, wd, ((1,), (0,))).astype(BF)
        part = (p * result.astype(F32)).astype(BF)
        return hidden, result, part

    def backward(c, p, pre):
        out_grad = (p * c.astype(F32)).astype(BF)
        hidden_grad = mm(out_grad, wd, ((1,), (1,)))
        gate, up = pre[:, :hid], pre[:, hid:]
        sig = jax.nn.sigmoid(gate)
        gate_grad = (hidden_grad * up * sig * (1.0 + gate * (1.0 - sig))).astype(BF)
        up_grad = (hidden_grad * (gate * sig)).astype(BF)
        pre_grad = jnp.concatenate([gate_grad, up_grad], axis=1)
        return lax.optimization_barrier((out_grad, pre_grad))

    def rowgrad(pre_grad):
        return lax.optimization_barrier(mm(pre_grad, wgu, ((1,), (1,))).astype(BF))

    q0, q1 = project(x0), project(x1)
    h1, r1, m1 = forward(q1, p1)
    h0, r0, m0 = forward(q0, p0)
    mixed = collect(m0, m1, rows)
    q0, h0, r0, q1, h1, r1 = lax.optimization_barrier((q0, h0, r0, q1, h1, r1))
    p0, p1 = lax.optimization_barrier((p0, p1))
    o0, g0 = backward(c0, p0, q0)
    o1, g1 = backward(c1, p1, q1)
    b1, b0 = rowgrad(g1), rowgrad(g0)
    t0, r0, t1, r1, _ = lax.optimization_barrier((c0, r0, c1, r1, b0))
    i0 = jnp.sum(t0.astype(F32) * r0.astype(F32), axis=1)
    i1 = jnp.sum(t1.astype(F32) * r1.astype(F32), axis=1)
    input_grad = shuffle(collect(b0, b1, rows))
    down_part = mm(h0, o0, ((0,), (0,))) + mm(h1, o1, ((0,), (0,)))
    down_part = (down_part * scale).astype(BF)
    down_parts = [down_part[j * dhid : (j + 1) * dhid] for j in range(data_devices)]
    down_parts = in_order(down_parts, own)
    down_grad = scatter_rows(down_parts)
    gu_part = mm(x0, g0, ((0,), (0,))) + mm(x1, g1, ((0,), (0,)))
    gu_part = (gu_part * scale).astype(BF)
    gu_grad = scatter_rows([gu_part[j * dwidth : (j + 1) * dwidth] for j in range(data_devices)])

    mine = i0.reshape(pairs, rows)
    other = send(i1.reshape(pairs, rows), "expert", 1)
    both = jnp.stack([mine, other], axis=1)
    prob_grad = jnp.zeros(expert_ids.shape, F32)
    for m in range(pairs):
        got = both[m] if m == 0 else send(both[m], "expert", 2 * m)
        for j in range(2):
            hit = expert_ids == (me ^ (2 * m + j))
            prob_grad = prob_grad + jnp.where(hit, got[j][:, None], 0.0)
    return (
        mixed,
        input_grad,
        prob_grad,
        gu_grad[None, :, :hid],
        gu_grad[None, :, hid:],
        down_grad[None],
    )


def solution(mesh):
    both = P(("dp", "expert"), None)
    weight = P("expert", "dp", None)
    return jax.shard_map(
        per_device,
        mesh=mesh,
        in_specs=(both, both, both, weight, weight, weight, both),
        out_specs=(both, both, both, weight, weight, weight),
        check_vma=False,
    )
```

```python
import jax
import jax.numpy as jnp
from jax import lax
from jax.sharding import PartitionSpec as P

BF = jnp.bfloat16
F32 = jnp.float32


def send(x, axis, flip, only=None):
    size = lax.axis_size(axis)
    pairs = [(j, j ^ flip) for j in range(size) if only is None or only(j, j ^ flip)]
    return lax.ppermute(x, axis, pairs)


def spread(block):
    pairs = lax.axis_size("expert") // 2
    if pairs == 4:
        inner = lambda a, b: a // 2 in (1, 2)
        two = send(block, "expert", 4)
        one = send(block, "expert", 2)
        mid = send(block, "expert", 6, inner)
        far = send(two, "expert", 2, lambda a, b: a // 2 in (1, 2))
        row = lax.axis_index("expert") // 2
        three = jnp.where((row == 1) | (row == 2), mid, far)
        mine = [block, one, two, three]
    else:
        mine = [block] + [send(block, "expert", 2 * m) for m in range(1, pairs)]
    mine = lax.optimization_barrier(jnp.concatenate(mine, axis=0))
    return mine, send(mine, "expert", 1)


def collect(mine, other, rows):
    pairs = lax.axis_size("expert") // 2
    got = send(other, "expert", 1)
    total = (mine.astype(F32) + got.astype(F32)).astype(BF)
    total = lax.optimization_barrier(total)
    parts = [total[m * rows : (m + 1) * rows] for m in range(pairs)]
    out = parts[0].astype(F32)
    for m in range(1, pairs):
        out = out + send(parts[m], "expert", 2 * m).astype(F32)
    return out.astype(BF)


def in_order(parts, own):
    parts = list(parts)
    step = 1
    while step < len(parts):
        odd = (own & step) != 0
        parts = [jnp.where(odd, parts[j ^ step], parts[j]) for j in range(len(parts))]
        step *= 2
    return parts


def gather_rows(shard):
    size = lax.axis_size("dp")
    if size > 8:
        full = lax.all_gather(shard, "dp", axis=0, tiled=False)
        own = lax.axis_index("dp")
        return [lax.dynamic_index_in_dim(full, own ^ m, 0, False) for m in range(size)]
    parts = [shard]
    for m in range(1, size if size != 4 else 3):
        parts.append(send(shard, "dp", m))
    if size == 4:
        half = shard.shape[0] // 2
        lo = send(parts[2][:half], "dp", 1)
        hi = send(parts[1][half:], "dp", 2)
        parts.append(jnp.concatenate([lo, hi], axis=0))
    return parts


def scatter_rows(parts):
    size = lax.axis_size("dp")
    if size > 8:
        whole = jnp.concatenate(in_order(parts, lax.axis_index("dp")))
        return lax.psum_scatter(whole, "dp", scatter_dimension=0, tiled=True)
    total = parts[0].astype(F32)
    for m in range(1, size):
        total = total + send(parts[m], "dp", m).astype(F32)
    return total.astype(BF)


def mm(a, b, dims):
    return lax.dot_general(a, b, ((dims[0], dims[1]), ((), ())), preferred_element_type=F32)


def per_device(tokens, expert_ids, gate_probs, w_gate, w_up, w_down, cotangent):
    rows, width = tokens.shape
    top = expert_ids.shape[1]
    hid = w_gate.shape[2]
    expert_devices = lax.axis_size("expert")
    data_devices = lax.axis_size("dp")
    pairs = expert_devices // 2
    experts = expert_devices
    assert w_gate.shape[0] == 1
    scale = (experts / (rows * top * data_devices * expert_devices)) ** 0.5
    me = lax.axis_index("expert")
    own = lax.axis_index("dp")
    dwidth = width // data_devices
    dhid = hid // data_devices

    def shuffle(x):
        cols = [x[:, j * dwidth : (j + 1) * dwidth] for j in range(data_devices)]
        return jnp.concatenate(in_order(cols, own), axis=1)

    chosen = expert_ids.T[None, :, :] == jnp.arange(experts, dtype=jnp.int32)[:, None, None]
    dense = jnp.sum(jnp.where(chosen, gate_probs.T[None, :, :], 0.0), axis=1)
    x0, x1 = spread(shuffle(tokens))
    pair = jnp.concatenate([w_gate[0], w_up[0]], axis=1)
    wgu = gather_rows(pair)
    wgu = lax.optimization_barrier(jnp.concatenate(wgu, axis=0))
    wd = gather_rows(w_down[0])
    wd = lax.optimization_barrier(jnp.concatenate(in_order(wd, own), axis=0))
    c0, c1 = spread(cotangent)
    near = [dense]
    for m in range(1, pairs):
        near.append(send(dense, "expert", 2 * m))
    near = lax.optimization_barrier(jnp.stack(near))
    far = send(near, "expert", 1)
    p0 = lax.dynamic_index_in_dim(near, me, 1, False).reshape(pairs * rows, 1)
    p1 = lax.dynamic_index_in_dim(far, me, 1, False).reshape(pairs * rows, 1)

    def project(x):
        return lax.optimization_barrier(mm(x, wgu, ((1,), (0,))))

    def forward(pre, p):
        hidden = (jax.nn.silu(pre[:, :hid]) * pre[:, hid:]).astype(BF)
        result = mm(hidden, wd, ((1,), (0,))).astype(BF)
        part = (p * result.astype(F32)).astype(BF)
        return hidden, result, part

    def backward(c, p, pre):
        out_grad = (p * c.astype(F32)).astype(BF)
        hidden_grad = mm(out_grad, wd, ((1,), (1,)))
        gate, up = pre[:, :hid], pre[:, hid:]
        sig = jax.nn.sigmoid(gate)
        gate_grad = (hidden_grad * up * sig * (1.0 + gate * (1.0 - sig))).astype(BF)
        up_grad = (hidden_grad * (gate * sig)).astype(BF)
        pre_grad = jnp.concatenate([gate_grad, up_grad], axis=1)
        return lax.optimization_barrier((out_grad, pre_grad))

    def rowgrad(pre_grad):
        return lax.optimization_barrier(mm(pre_grad, wgu, ((1,), (1,))).astype(BF))

    q0, q1 = project(x0), project(x1)
    h1, r1, m1 = forward(q1, p1)
    h0, r0, m0 = forward(q0, p0)
    mixed = collect(m0, m1, rows)
    q0, h0, r0, q1, h1, r1 = lax.optimization_barrier((q0, h0, r0, q1, h1, r1))
    p0, p1 = lax.optimization_barrier((p0, p1))
    o0, g0 = backward(c0, p0, q0)
    o1, g1 = backward(c1, p1, q1)
    b1, b0 = rowgrad(g1), rowgrad(g0)
    t0, r0, t1, r1, _ = lax.optimization_barrier((c0, r0, c1, r1, g1))
    i0 = jnp.sum(t0.astype(F32) * r0.astype(F32), axis=1)
    i1 = jnp.sum(t1.astype(F32) * r1.astype(F32), axis=1)
    input_grad = shuffle(collect(b0, b1, rows))
    down_part = mm(h0, o0, ((0,), (0,))) + mm(h1, o1, ((0,), (0,)))
    down_part = (down_part * scale).astype(BF)
    down_parts = [down_part[j * dhid : (j + 1) * dhid] for j in range(data_devices)]
    down_parts = in_order(down_parts, own)
    down_grad = scatter_rows(down_parts)
    gu_parts = []
    for m in range(data_devices):
        cols = slice(m * dwidth, (m + 1) * dwidth)
        part = mm(x0[:, cols], g0, ((0,), (0,))) + mm(x1[:, cols], g1, ((0,), (0,)))
        gu_parts.append(lax.optimization_barrier((part * scale).astype(BF)))
    gu_grad = scatter_rows(gu_parts)

    mine = i0.reshape(pairs, rows)
    other = send(i1.reshape(pairs, rows), "expert", 1)
    both = jnp.stack([mine, other], axis=1)
    prob_grad = jnp.zeros(expert_ids.shape, F32)
    for m in range(pairs):
        got = both[m] if m == 0 else send(both[m], "expert", 2 * m)
        for j in range(2):
            hit = expert_ids == (me ^ (2 * m + j))
            prob_grad = prob_grad + jnp.where(hit, got[j][:, None], 0.0)
    return (
        mixed,
        input_grad,
        prob_grad,
        gu_grad[None, :, :hid],
        gu_grad[None, :, hid:],
        down_grad[None],
    )


def solution(mesh):
    both = P(("dp", "expert"), None)
    weight = P("expert", "dp", None)
    return jax.shard_map(
        per_device,
        mesh=mesh,
        in_specs=(both, both, both, weight, weight, weight, both),
        out_specs=(both, both, both, weight, weight, weight),
        check_vma=False,
    )
```

```python
import jax
import jax.numpy as jnp
from jax import lax
from jax.sharding import PartitionSpec as P

BF = jnp.bfloat16
F32 = jnp.float32


def send(x, axis, flip, only=None):
    size = lax.axis_size(axis)
    pairs = [(j, j ^ flip) for j in range(size) if only is None or only(j, j ^ flip)]
    return lax.ppermute(x, axis, pairs)


def block_order(pairs):
    order, step = [0], pairs // 2
    while step:
        order, step = order + [a ^ step for a in order], step // 2
    return order


def spread(block, arrange=lambda x: x):
    pairs = lax.axis_size("expert") // 2
    if pairs == 4:
        inner = lambda a, b: a // 2 in (1, 2)
        two = send(block, "expert", 4)
        one = send(block, "expert", 2)
        mid = send(block, "expert", 6, inner)
        far = send(two, "expert", 2, inner)
        row = lax.axis_index("expert") // 2
        three = jnp.where((row == 1) | (row == 2), mid, far)
        mine = [block, two, one, three]
    else:
        mine = [block] + [send(block, "expert", 2 * m) for m in block_order(pairs)[1:]]
    mine = lax.optimization_barrier(arrange(jnp.concatenate(mine, axis=0)))
    return mine, send(mine, "expert", 1)


def collect(mine, other):
    pairs = lax.axis_size("expert") // 2
    got = send(other, "expert", 1)
    total = (mine.astype(F32) + got.astype(F32)).astype(BF)
    total = lax.optimization_barrier(total)
    step = 1
    while step < pairs:
        half = total.shape[0] // 2
        got = send(total[half:], "expert", 2 * step)
        total = (total[:half].astype(F32) + got.astype(F32)).astype(BF)
        step *= 2
    return total


def in_order(parts, own):
    parts = list(parts)
    step = 1
    while step < len(parts):
        odd = (own & step) != 0
        parts = [jnp.where(odd, parts[j ^ step], parts[j]) for j in range(len(parts))]
        step *= 2
    return parts


def gather_rows(shard):
    size = lax.axis_size("dp")
    if size > 8:
        full = lax.all_gather(shard, "dp", axis=0, tiled=False)
        own = lax.axis_index("dp")
        return [lax.dynamic_index_in_dim(full, own ^ m, 0, False) for m in range(size)]
    parts = [shard]
    for m in range(1, size if size != 4 else 3):
        parts.append(send(shard, "dp", m))
    if size == 4:
        half = shard.shape[0] // 2
        lo = send(parts[2][:half], "dp", 1)
        hi = send(parts[1][half:], "dp", 2)
        parts.append(jnp.concatenate([lo, hi], axis=0))
    return parts


def scatter_rows(parts):
    size = lax.axis_size("dp")
    if size > 8:
        whole = jnp.concatenate(in_order(parts, lax.axis_index("dp")))
        return lax.psum_scatter(whole, "dp", scatter_dimension=0, tiled=True)
    total = parts[0].astype(F32)
    for m in range(1, size):
        total = total + send(parts[m], "dp", m).astype(F32)
    return total.astype(BF)


def mm(a, b, dims):
    return lax.dot_general(a, b, ((dims[0], dims[1]), ((), ())), preferred_element_type=F32)


def per_device(tokens, expert_ids, gate_probs, w_gate, w_up, w_down, cotangent):
    rows, width = tokens.shape
    top = expert_ids.shape[1]
    hid = w_gate.shape[2]
    expert_devices = lax.axis_size("expert")
    data_devices = lax.axis_size("dp")
    pairs = expert_devices // 2
    experts = expert_devices
    assert w_gate.shape[0] == 1
    scale = (experts / (rows * top * data_devices * expert_devices)) ** 0.5
    me = lax.axis_index("expert")
    own = lax.axis_index("dp")
    dwidth = width // data_devices
    dhid = hid // data_devices

    def shuffle(x):
        cols = [x[:, j * dwidth : (j + 1) * dwidth] for j in range(data_devices)]
        return jnp.concatenate(in_order(cols, own), axis=1)

    chosen = expert_ids.T[None, :, :] == jnp.arange(experts, dtype=jnp.int32)[:, None, None]
    dense = jnp.sum(jnp.where(chosen, gate_probs.T[None, :, :], 0.0), axis=1)
    x0, x1 = spread(tokens, shuffle)
    pair = jnp.concatenate([w_gate[0], w_up[0]], axis=1)
    wgu = gather_rows(pair)
    wgu = lax.optimization_barrier(jnp.concatenate(wgu, axis=0))
    wd = gather_rows(w_down[0])
    wd = lax.optimization_barrier(jnp.concatenate(in_order(wd, own), axis=0))
    c0, c1 = spread(cotangent)
    near = [dense]
    for m in block_order(pairs)[1:]:
        near.append(send(dense, "expert", 2 * m))
    near = lax.optimization_barrier(jnp.stack(near))
    far = send(near, "expert", 1)
    p0 = lax.dynamic_index_in_dim(near, me, 1, False).reshape(pairs * rows, 1)
    p1 = lax.dynamic_index_in_dim(far, me, 1, False).reshape(pairs * rows, 1)

    def project(x):
        return lax.optimization_barrier(mm(x, wgu, ((1,), (0,))))

    def forward(pre, p):
        hidden = (jax.nn.silu(pre[:, :hid]) * pre[:, hid:]).astype(BF)
        result = mm(hidden, wd, ((1,), (0,))).astype(BF)
        part = (p * result.astype(F32)).astype(BF)
        return hidden, result, part

    def backward(c, p, pre):
        out_grad = (p * c.astype(F32)).astype(BF)
        hidden_grad = mm(out_grad, wd, ((1,), (1,)))
        gate, up = pre[:, :hid], pre[:, hid:]
        sig = jax.nn.sigmoid(gate)
        gate_grad = (hidden_grad * up * sig * (1.0 + gate * (1.0 - sig))).astype(BF)
        up_grad = (hidden_grad * (gate * sig)).astype(BF)
        pre_grad = jnp.concatenate([gate_grad, up_grad], axis=1)
        return lax.optimization_barrier((out_grad, pre_grad))

    def rowgrad(pre_grad):
        return lax.optimization_barrier(mm(pre_grad, wgu, ((1,), (1,))).astype(BF))

    q0, q1 = project(x0), project(x1)
    h1, r1, m1 = forward(q1, p1)
    h0, r0, m0 = forward(q0, p0)
    mixed = collect(m0, m1)
    q0, h0, r0, q1, h1, r1 = lax.optimization_barrier((q0, h0, r0, q1, h1, r1))
    p0, p1 = lax.optimization_barrier((p0, p1))
    o0, g0 = backward(c0, p0, q0)
    o1, g1 = backward(c1, p1, q1)
    b1, b0 = rowgrad(g1), rowgrad(g0)
    t0, r0, t1, r1, _ = lax.optimization_barrier((c0, r0, c1, r1, g1))
    i0 = jnp.sum(t0.astype(F32) * r0.astype(F32), axis=1)
    i1 = jnp.sum(t1.astype(F32) * r1.astype(F32), axis=1)
    input_grad = shuffle(collect(b0, b1))
    down_part = mm(h0, o0, ((0,), (0,))) + mm(h1, o1, ((0,), (0,)))
    down_part = (down_part * scale).astype(BF)
    down_parts = [down_part[j * dhid : (j + 1) * dhid] for j in range(data_devices)]
    down_parts = in_order(down_parts, own)
    down_grad = scatter_rows(down_parts)
    gu_parts = []
    for m in range(data_devices):
        cols = slice(m * dwidth, (m + 1) * dwidth)
        part = mm(x0[:, cols], g0, ((0,), (0,))) + mm(x1[:, cols], g1, ((0,), (0,)))
        gu_parts.append(lax.optimization_barrier((part * scale).astype(BF)))
    gu_grad = scatter_rows(gu_parts)

    mine = i0.reshape(pairs, rows)
    other = send(i1.reshape(pairs, rows), "expert", 1)
    found, source, step = jnp.stack([mine, other], axis=1)[None], [0], 1
    while step < pairs:
        half = found.shape[1] // 2
        got = send(found[:, half:], "expert", 2 * step)
        found = jnp.concatenate([found[:, :half], got], axis=0)
        source, step = source + [a ^ step for a in source], 2 * step
    prob_grad = jnp.zeros(expert_ids.shape, F32)
    for at, m in enumerate(source):
        for j in range(2):
            hit = expert_ids == (me ^ (2 * m + j))
            prob_grad = prob_grad + jnp.where(hit, found[at, 0, j][:, None], 0.0)
    return (
        mixed,
        input_grad,
        prob_grad,
        gu_grad[None, :, :hid],
        gu_grad[None, :, hid:],
        down_grad[None],
    )


def solution(mesh):
    both = P(("dp", "expert"), None)
    weight = P("expert", "dp", None)
    return jax.shard_map(
        per_device,
        mesh=mesh,
        in_specs=(both, both, both, weight, weight, weight, both),
        out_specs=(both, both, both, weight, weight, weight),
        check_vma=False,
    )
```
